256 devices in a mesh: src: 64 (over z, x, y_lo), tgt: 4 (over y_hi, core).
Axes of the slice: x: 4, y: 4 (y_hi: 2, y_lo: 2; y = y_hi * 2 + y_lo), z: 8, core: 2. Of those that a mesh axis runs over, the one named last changes fastest.
Arguments:
- src_feat: bfloat16 [131072, 768], P(('src', 'tgt')), may hold values from -6 to 6
- tgt_feat: bfloat16 [8192, 768], P(('tgt', 'src')), may hold values from -6 to 6
- rel_weight: bfloat16 [3, 768, 1024], replicated, may hold values from -0.21875 to 0.21875
- self_weight: bfloat16 [768, 1024], replicated, may hold values from -0.21875 to 0.21875
- adj_weight: bfloat16 [64, 64, 4, 128, 128], P('src', 'tgt'), may hold values from 0 to 0.009521484
- adj_source: int32 [64, 64, 4], P('src', 'tgt'), may hold values from 0 to 47
- adj_count: int32 [64, 64], P('src', 'tgt'), may hold values from 1 to 4
Outputs:
- hidden_out: bfloat16 [8192, 1024], P(('tgt', 'src'))
The draws below stay inside these ranges and needn't reach their ends.
All inputs are finite; a program needn't handle non-finite values.
Results may differ from the reference program's by a relative error of at most 0.004.
Values may be sent and summed in bfloat16 or wider, within the bound.
No kernel may reach another device: no remote copies, remote signals or barrier semaphores. Data moves between devices by JAX's collectives and lax.ppermute only.
A program may use at most 128 MiB of HBM per device.

```python
import math
import jax
import jax.numpy as jnp
import numpy as np
from jax import lax

D = 768
HID = 1024
REL = 3
BLK = 128
KSLOT = 4
SRC_DEV = 2048
SOURCES = 131072
TBLOCKS = 64
TARGETS = 8192
N_SRC = 64


def plant(array, own_key, least, largest):
    spot = [jax.random.randint(jax.random.fold_in(own_key, axis), (), 0, length) for axis, length in enumerate(array.shape)]
    longest = array.shape.index(max(array.shape))
    beside = spot[:longest] + [(spot[longest] + 1) % array.shape[longest]] + spot[longest + 1:]
    return array.at[tuple(spot)].set(least).at[tuple(beside)].set(largest)


def shard_levels(key, extent, shards, smallest, top_value):
    loudness, own = 1.0, jax.random.fold_in(key, 6)
    for position, blocks in shards:
        steps = jnp.exp(jax.random.uniform(jax.random.fold_in(own, position), (blocks,), jnp.float32, smallest / len(shards), top_value / len(shards)))
        loudness = loudness * jnp.repeat(steps, extent[position] // blocks).reshape([-1 if axis == position else 1 for axis in range(len(extent))])
    return loudness


def cumulative_ranks(count, skew):
    weights = [(1 << 20) // math.isqrt(standing ** skew) + 1 for standing in range(1, count + 1)]
    spread = 1 + sum(weights) // (1 << 30)
    return np.cumsum(np.array([max(1, weight // spread) for weight in weights]))


def skewed_ids(key, shape, number_of, slope):
    grid = cumulative_ranks(number_of, slope)
    pick = jax.random.randint(jax.random.fold_in(key, 1), shape, 0, int(grid[number_of - 1]))
    rank = jnp.searchsorted(jnp.asarray(grid, jnp.int32), pick, side="right")
    return jax.random.permutation(jax.random.fold_in(key, 2), number_of)[rank].astype(jnp.int32)


def scatter_about(rng, dims, scale, most, split=(), kind=jnp.bfloat16):
    values = jax.random.normal(rng, dims, jnp.float32) * scale
    if len(split) > 0:
        values = shard_levels(rng, dims, split, -0.22, 0.18) * values
    return jnp.clip(values, min=-most, max=most).astype(kind)


def setup_inputs(seed: int = 0) -> dict:
    splits = jax.random.split(jax.random.key(seed), 8)
    src_feat = scatter_about(splits[0], (SOURCES, D), 1.0, 6.0, ((0, 256),))
    tgt_feat = scatter_about(splits[1], (TARGETS, D), 1.0, 6.0, ((0, 256),))
    rel_weight = scatter_about(splits[2], (REL, D, HID), D ** -0.5, 0.21875)
    self_weight = scatter_about(splits[3], (D, HID), D ** -0.5, 0.21875)
    adj_weight = jnp.clip(0.009521484 * jax.random.uniform(splits[4], (N_SRC, TBLOCKS, KSLOT, BLK, BLK), jnp.float32) ** shard_levels(splits[4], (N_SRC, TBLOCKS, KSLOT, BLK, BLK), ((0, 64), (1, 4)), -0.2, 0.2), 0.0, 0.009521484).astype(jnp.bfloat16)
    adj_source = plant(skewed_ids(splits[5], (N_SRC, TBLOCKS, KSLOT), REL * SRC_DEV // BLK, 2), jax.random.fold_in(splits[5], 3), 0, (REL * SRC_DEV // BLK) - 1).astype(jnp.int32)
    adj_count = plant(jax.random.randint(splits[6], (N_SRC, TBLOCKS), 1, KSLOT + 1), jax.random.fold_in(splits[6], 1), 1, KSLOT).astype(jnp.int32)
    return dict(src_feat=src_feat, tgt_feat=tgt_feat, rel_weight=rel_weight, self_weight=self_weight, adj_weight=adj_weight, adj_source=adj_source, adj_count=adj_count)


def reference(src_feat, tgt_feat, rel_weight, self_weight, adj_weight, adj_source, adj_count):
    features = src_feat.reshape(N_SRC, SRC_DEV, D)
    slot_iota = jnp.arange(KSLOT, dtype=jnp.int32)

    def per_device(running, inputs):
        src_rows, weights, source_index, count_live = inputs
        transformed = jnp.einsum("nd,rdh->rnh", src_rows.astype(jnp.float32), rel_weight.astype(jnp.float32)).astype(jnp.bfloat16)
        transformed = transformed.reshape(REL * (SRC_DEV // BLK), BLK, HID)
        picked = transformed[source_index]
        alive_mask = slot_iota[None, :] < count_live[:, None]
        live_weight = jnp.where(alive_mask[:, :, None, None], weights, jnp.zeros_like(weights))
        partial_value = jnp.einsum("tkij,tkjh->tih", live_weight.astype(jnp.float32), picked.astype(jnp.float32))
        return running + partial_value, None

    start = jnp.zeros((TBLOCKS, BLK, HID), jnp.float32)
    summed, _ = lax.scan(per_device, start, (features, adj_weight, adj_source, adj_count))
    summed = summed.reshape(TARGETS, HID)
    self_term = jnp.dot(tgt_feat, self_weight, preferred_element_type=jnp.float32)
    return jax.nn.relu(summed + self_term).astype(jnp.bfloat16)
```

```python
import jax
import jax.numpy as jnp
from jax import lax
from jax.experimental import pallas as pl
from jax.experimental.pallas import tpu as pltpu
from jax.sharding import Mesh, PartitionSpec as P

HID = 1024
BLK = 128
REL = 3
NZ, NX, NY = 8, 4, 2
HA = 384
F32 = jnp.float32
BF16 = jnp.bfloat16


def transform_rows(f_ref, w_ref, t_ref, base):
    n = f_ref.shape[0] // BLK
    pairs = n // 2

    def step(i, _):
        r = i // pairs
        p = i - r * pairs
        y = jnp.dot(f_ref[pl.ds(p * 2 * BLK, 2 * BLK), :], w_ref[r], preferred_element_type=F32)
        t_ref[pl.ds(base + r * n + p * 2, 2)] = y.astype(BF16).reshape(2, BLK, HID)
        return 0

    lax.fori_loop(0, REL * pairs, step, 0)


def transform_kernel(f_ref, w_ref, t_ref):
    transform_rows(f_ref, w_ref, t_ref, 0)


def transform(feat, weight):
    n = REL * feat.shape[0] // BLK
    return pl.pallas_call(
        transform_kernel,
        out_shape=jax.ShapeDtypeStruct((n, BLK, HID), BF16),
        compiler_params=pltpu.CompilerParams(vmem_limit_bytes=40 << 20),
        cost_estimate=pl.CostEstimate(
            flops=2 * feat.size * HID * REL, transcendentals=0, bytes_accessed=12 << 20
        ),
    )(feat, weight)


def aggregate_kernel(src_ref, cnt_ref, me_ref, t0_ref, t1_ref, t2_ref, f_ref, w_ref, adj_ref, a_ref, b_ref, t_ref, sems):
    copies = [
        pltpu.make_async_copy(part, t_ref.at[pl.ds(12 * q, 12)], sems.at[q])
        for q, part in enumerate((t0_ref, t1_ref, t2_ref))
    ]
    for copy in copies:
        copy.start()
    transform_rows(f_ref, w_ref, t_ref, 36)
    for copy in copies:
        copy.wait()
    slots = adj_ref.shape[1]
    me = me_ref[0]

    def step(t, _):
        weights, picked = [], []
        for k in range(slots):
            v = src_ref[t * slots + k]
            r = lax.shift_right_logical(v, 4)
            j = lax.bitwise_and(v, 15)
            q = lax.bitwise_xor(lax.shift_right_logical(j, 2), me)
            block = q * 12 + r * 4 + lax.bitwise_and(j, 3)
            w = adj_ref[t, k]
            weights.append(jnp.where(k < cnt_ref[t], w, jnp.zeros_like(w)))
            picked.append(t_ref[block])
        acc = jnp.dot(
            jnp.concatenate(weights, axis=1), jnp.concatenate(picked, axis=0), preferred_element_type=F32
        ).astype(BF16)
        half = lax.shift_right_logical(t, 1)
        odd = lax.bitwise_and(t, 1)
        a_ref[half, pl.ds(odd * BLK, BLK), :] = acc[:, :HA]
        for u in range(4):
            b_ref[odd * 4 + u, pl.ds(half * 32, 32), :] = acc[u * 32 : (u + 1) * 32, HA:]
        return 0

    lax.fori_loop(0, adj_ref.shape[0], step, 0)


def aggregate(src, cnt, me, parts, feat, weight, adj):
    smem = pl.BlockSpec(memory_space=pltpu.SMEM)
    vmem = pl.BlockSpec(memory_space=pltpu.VMEM)
    hbm = pl.BlockSpec(memory_space=pl.ANY)
    return pl.pallas_call(
        aggregate_kernel,
        out_shape=(
            jax.ShapeDtypeStruct((NZ, 256, HA), BF16),
            jax.ShapeDtypeStruct((NX * NY, 256, HID - HA), BF16),
        ),
        in_specs=[smem, smem, smem, hbm, hbm, hbm, vmem, vmem, vmem],
        out_specs=(vmem, vmem),
        scratch_shapes=[pltpu.VMEM((48, BLK, HID), BF16), pltpu.SemaphoreType.DMA((3,))],
        compiler_params=pltpu.CompilerParams(vmem_limit_bytes=48 << 20),
    )(src, cnt, me, *parts, feat, weight, adj)


def exchange(x, axes):
    return lax.all_to_all(x, axes, 0, 0, tiled=True)


def shards(src_feat, tgt_feat, rel_weight, self_weight, adj_weight, adj_source, adj_count):
    swap = [(0, 1), (1, 0)]
    far = lax.ppermute(src_feat, "yh", swap)
    near = lax.ppermute(src_feat, "core", swap)
    diag = lax.ppermute(far, "core", swap)
    me = (lax.axis_index("yh") * 2 + lax.axis_index("core")).astype(jnp.int32).reshape(1)
    parts = [transform(f, rel_weight) for f in (src_feat, near, far)]
    out_a, out_b = aggregate(
        adj_source.reshape(-1), adj_count.reshape(-1), me, parts, diag, rel_weight, adj_weight[0]
    )
    got_a = exchange(out_a, "z")
    got_b = exchange(out_b, ("x", "yl"))
    sum_a = got_a.astype(F32).sum(0).astype(BF16).reshape(NX * NY, 32, HA)
    sum_b = got_b.astype(F32).sum(0).astype(BF16).reshape(NZ, 32, HID - HA)
    last_a = exchange(sum_a, ("x", "yl"))
    last_b = exchange(sum_b, "z")
    summed = jnp.concatenate([last_a.astype(F32).sum(0), last_b.astype(F32).sum(0)], axis=1)
    self_term = jnp.dot(tgt_feat, self_weight, preferred_element_type=F32)
    return jax.nn.relu(summed + self_term).astype(BF16)


def solution(mesh):
    fine = Mesh(mesh.devices.reshape(NZ, NX, NY, 2, 2), ("z", "x", "yl", "yh", "core"))
    src, tgt = ("z", "x", "yl"), ("yh", "core")
    return jax.shard_map(
        shards,
        mesh=fine,
        in_specs=(
            P(src + tgt, None),
            P(tgt + src, None),
            P(),
            P(),
            P(src, tgt, None, None, None),
            P(src, tgt, None),
            P(src, tgt),
        ),
        out_specs=P(tgt + src, None),
        check_vma=False,
    )
```

```python
import jax
import jax.numpy as jnp
from jax import lax
from jax.experimental import pallas as pl
from jax.experimental.pallas import tpu as pltpu
from jax.sharding import Mesh, PartitionSpec as P


HID = 1024
BLK = 128
REL = 3
NZ, NX, NY = 8, 4, 2
ROWS = 32
HA = 384
HB = HID - HA
PART = 12
F32 = jnp.float32
BF16 = jnp.bfloat16
SMEM = pl.BlockSpec(memory_space=pltpu.SMEM)
VMEM = pl.BlockSpec(memory_space=pltpu.VMEM)
HOPS = [(dx, dy) for dx in range(NX) for dy in range(NY)]


def transform_rows(f_ref, w_ref, cols, store):
    n = f_ref.shape[0] // BLK
    pairs = n // 2

    def step(i, _):
        r = i // pairs
        p = i - r * pairs
        y = jnp.dot(f_ref[pl.ds(p * 2 * BLK, 2 * BLK), :], w_ref[r, :, cols], preferred_element_type=F32)
        store(r * n + p * 2, y.astype(BF16).reshape(2, BLK, y.shape[1]))
        return 0

    lax.fori_loop(0, REL * pairs, step, 0)


def transform_kernel(f_ref, w_ref, ta_ref, tb_ref):
    def store(at, blocks):
        ta_ref[pl.ds(at, 2)] = blocks[:, :, :HA]
        tb_ref[pl.ds(at, 2)] = blocks[:, :, HA:]

    transform_rows(f_ref, w_ref, slice(0, HID), store)


def transform(feat, weight):
    return pl.pallas_call(
        transform_kernel,
        out_shape=tuple(jax.ShapeDtypeStruct((PART, BLK, n), BF16) for n in (HA, HB)),
        in_specs=[VMEM, VMEM],
        out_specs=(VMEM, VMEM),
        compiler_params=pltpu.CompilerParams(vmem_limit_bytes=24 << 20),
        cost_estimate=pl.CostEstimate(
            flops=2 * feat.size * HID * REL, transcendentals=0, bytes_accessed=8 << 20
        ),
    )(feat, weight)


def fill_table(parts, f_ref, w_ref, t_ref, sems, cols):
    copies = [
        pltpu.make_async_copy(part, t_ref.at[pl.ds(PART * q, PART)], sems.at[q]) for q, part in enumerate(parts)
    ]
    for copy in copies:
        copy.start()

    def store(at, blocks):
        t_ref[pl.ds(PART * len(parts) + at, 2)] = blocks

    transform_rows(f_ref, w_ref, cols, store)
    for copy in copies:
        copy.wait()


def weighted_sum(t, src_ref, cnt_ref, me, adj_ref, t_ref):
    slots = adj_ref.shape[1]
    weights, picked = [], []
    for k in range(slots):
        v = src_ref[t * slots + k]
        r = lax.shift_right_logical(v, 4)
        j = lax.bitwise_and(v, 15)
        q = lax.bitwise_xor(lax.shift_right_logical(j, 2), me)
        w = adj_ref[t, k]
        weights.append(jnp.where(k < cnt_ref[t], w, jnp.zeros_like(w)))
        picked.append(t_ref[q * PART + r * 4 + lax.bitwise_and(j, 3)])
    return jnp.dot(
        jnp.concatenate(weights, axis=1), jnp.concatenate(picked, axis=0), preferred_element_type=F32
    ).astype(BF16)


def sum_a_kernel(src_ref, cnt_ref, pos_ref, f_ref, w_ref, adj_ref, p0, p1, p2, a_ref, t_ref, sems):
    fill_table((p0, p1, p2), f_ref, w_ref, t_ref, sems, slice(0, HA))

    def step(t, _):
        got = weighted_sum(t, src_ref, cnt_ref, pos_ref[0], adj_ref, t_ref)
        a_ref[pl.ds(pl.multiple_of(t * BLK, BLK), BLK), :] = got
        return 0

    lax.fori_loop(0, adj_ref.shape[0], step, 0)


def hop_rows(pos_ref, dx, dy):
    x = lax.bitwise_and(pos_ref[1] + dx, NX - 1)
    y = lax.bitwise_xor(pos_ref[2], dy)
    return pl.multiple_of((x * NY + y) * ROWS, ROWS)


def sum_b_kernel(src_ref, cnt_ref, pos_ref, f_ref, w_ref, adj_ref, p0, p1, p2, *refs):
    b_refs, both, t_ref, sems = refs[:-3], refs[-3], refs[-2], refs[-1]
    fill_table((p0, p1, p2), f_ref, w_ref, t_ref, sems, slice(HA, HID))

    def step(z, _):
        for odd in range(2):
            both[odd * BLK : (odd + 1) * BLK, :] = weighted_sum(
                z * 2 + odd, src_ref, cnt_ref, pos_ref[0], adj_ref, t_ref
            )
        for (dx, dy), b_ref in zip(HOPS, b_refs):
            b_ref[pl.ds(pl.multiple_of(z * ROWS, ROWS), ROWS), :] = both[pl.ds(hop_rows(pos_ref, dx, dy), ROWS), :]
        return 0

    lax.fori_loop(0, NZ, step, 0)


def aggregate(kernel, outs, width, scratch, small, parts):
    return pl.pallas_call(
        kernel,
        out_shape=outs,
        in_specs=[SMEM] * 3 + [VMEM] * 3 + [pl.BlockSpec(memory_space=pl.ANY)] * 3,
        out_specs=jax.tree.map(lambda _: VMEM, outs),
        scratch_shapes=scratch
        + [pltpu.VMEM((4 * PART, BLK, width), BF16), pltpu.SemaphoreType.DMA((3,))],
        compiler_params=pltpu.CompilerParams(vmem_limit_bytes=32 << 20),
        cost_estimate=pl.CostEstimate(flops=6 * width << 20, transcendentals=0, bytes_accessed=16 << 20),
    )(*small, *parts)


def exchange(x, axes):
    return lax.all_to_all(x, axes, 0, 0, tiled=True)


def hop(x, dx, dy):
    pairs = [(i * NY + j, (i + dx) % NX * NY + (j ^ dy)) for i in range(NX) for j in range(NY)]
    return lax.ppermute(x, ("x", "yl"), pairs)


def layer(src_feat, tgt_feat, rel_weight, self_weight, adj_weight, adj_source, adj_count):
    swap = [(0, 1), (1, 0)]
    far = lax.ppermute(src_feat, "yh", swap)
    near = lax.ppermute(src_feat, "core", swap)
    diag = lax.ppermute(far, "core", swap)
    pos = jnp.stack(
        [lax.axis_index("yh") * 2 + lax.axis_index("core"), lax.axis_index("x"), lax.axis_index("yl")]
    ).astype(jnp.int32)
    parts = []
    for feat in (src_feat, near, far):
        parts.append(transform(feat, rel_weight))
    small = (adj_source.reshape(-1), adj_count.reshape(-1), pos, diag, rel_weight, adj_weight[0])
    outs = jax.ShapeDtypeStruct((NZ * 256, HA), BF16)
    out_a = aggregate(sum_a_kernel, outs, HA, [], small, [p[0] for p in parts])
    outs = tuple(jax.ShapeDtypeStruct((256, HB), BF16) for _ in HOPS)
    out_b = aggregate(sum_b_kernel, outs, HB, [pltpu.VMEM((256, HB), BF16)], small, [p[1] for p in parts])
    got_a = exchange(out_a.reshape(NZ, 256, HA), "z")
    got_b = [out_b[0]] + [hop(b, dx, dy) for b, (dx, dy) in zip(out_b[1:], HOPS[1:])]
    sum_a = got_a.astype(F32).sum(0).astype(BF16).reshape(NX * NY, ROWS, HA)
    sum_b = sum(b.astype(F32) for b in got_b).astype(BF16).reshape(NZ, ROWS, HB)
    last_a = exchange(sum_a, ("x", "yl"))
    last_b = exchange(sum_b, "z")
    end_a = last_a.astype(F32).sum(0)
    end_b = last_b.astype(F32).sum(0)
    summed = jnp.concatenate([end_a, end_b], axis=1)
    self_term = jnp.dot(tgt_feat, self_weight, preferred_element_type=F32)
    return jax.nn.relu(summed + self_term).astype(BF16)


def solution(mesh):
    fine = Mesh(mesh.devices.reshape(NZ, NX, NY, 2, 2), ("z", "x", "yl", "yh", "core"))
    src, tgt = ("z", "x", "yl"), ("yh", "core")
    return jax.shard_map(
        layer,
        mesh=fine,
        in_specs=(
            P(src + tgt, None),
            P(tgt + src, None),
            P(),
            P(),
            P(src, tgt, None, None, None),
            P(src, tgt, None),
            P(src, tgt),
        ),
        out_specs=P(tgt + src, None),
        check_vma=False,
    )
```

```python
import jax
import jax.numpy as jnp
from jax import lax
from jax.experimental import pallas as pl
from jax.experimental.pallas import tpu as pltpu
from jax.sharding import Mesh, PartitionSpec as P


HID = 1024
BLK = 128
REL = 3
NZ, NX, NY = 8, 4, 2
ROWS = 32
HA = 384
HB = HID - HA
PART = 12
F32 = jnp.float32
BF16 = jnp.bfloat16
SMEM = pl.BlockSpec(memory_space=pltpu.SMEM)
VMEM = pl.BlockSpec(memory_space=pltpu.VMEM)
HOPS = [(0, 0), (2, 1), (2, 0), (1, 1), (3, 1), (1, 0), (3, 0), (0, 1)]


def transform_rows(f_ref, w_ref, t_ref, base):
    n = f_ref.shape[0] // BLK
    pairs = n // 2

    def step(i, _):
        r = i // pairs
        p = i - r * pairs
        y = jnp.dot(f_ref[pl.ds(p * 2 * BLK, 2 * BLK), :], w_ref[r], preferred_element_type=F32)
        t_ref[pl.ds(base + r * n + p * 2, 2)] = y.astype(BF16).reshape(2, BLK, HID)
        return 0

    lax.fori_loop(0, REL * pairs, step, 0)


def transform_kernel(f_ref, w_ref, t_ref):
    transform_rows(f_ref, w_ref, t_ref, 0)


def transform(feat, weight):
    return pl.pallas_call(
        transform_kernel,
        out_shape=jax.ShapeDtypeStruct((PART, BLK, HID), BF16),
        in_specs=[VMEM, VMEM],
        out_specs=VMEM,
        compiler_params=pltpu.CompilerParams(vmem_limit_bytes=8 << 20),
        cost_estimate=pl.CostEstimate(
            flops=2 * feat.size * HID * REL, transcendentals=0, bytes_accessed=8 << 20
        ),
    )(feat, weight)


def weighted_sum(t, src_ref, cnt_ref, me, adj_ref, t_ref):
    weights, picked = [], []
    for k in range(adj_ref.shape[1]):
        v = src_ref[k, t]
        r = lax.shift_right_logical(v, 4)
        j = lax.bitwise_and(v, 15)
        q = lax.bitwise_xor(lax.shift_right_logical(j, 2), me)
        w = adj_ref[t, k]
        weights.append(jnp.where(k < cnt_ref[0, t], w, jnp.zeros_like(w)))
        picked.append(t_ref[q * PART + r * 4 + lax.bitwise_and(j, 3)])
    return jnp.dot(
        jnp.concatenate(weights, axis=1), jnp.concatenate(picked, axis=0), preferred_element_type=F32
    ).astype(BF16)


def aggregate_kernel(src_ref, cnt_ref, f_ref, w_ref, adj_ref, p0, p1, p2, a_ref, *refs):
    b_refs, both, t_ref, sems = refs[:-3], refs[-3], refs[-2], refs[-1]
    copies = [
        pltpu.make_async_copy(part, t_ref.at[pl.ds(PART * q, PART)], sems.at[q])
        for q, part in enumerate((p0, p1, p2))
    ]
    for copy in copies:
        copy.start()
    transform_rows(f_ref, w_ref, t_ref, PART * len(copies))
    for copy in copies:
        copy.wait()
    me = lax.axis_index("yh") * 2 + lax.axis_index("core")
    x0, y0 = lax.axis_index("x"), lax.axis_index("yl")

    def step(z, _):
        for odd in range(2):
            got = weighted_sum(z * 2 + odd, src_ref, cnt_ref, me, adj_ref, t_ref)
            a_ref[z, odd * BLK : (odd + 1) * BLK, :] = got[:, :HA]
            both[odd * BLK : (odd + 1) * BLK, :] = got[:, HA:]
        for (dx, dy), b_ref in zip(HOPS, b_refs):
            to = lax.bitwise_and(x0 + dx, NX - 1) * NY + lax.bitwise_xor(y0, dy)
            rows = both[pl.ds(pl.multiple_of(to * ROWS, ROWS), ROWS), :]
            b_ref[pl.ds(pl.multiple_of(z * ROWS, ROWS), ROWS), :] = rows
        return 0

    lax.fori_loop(0, NZ, step, 0)


def aggregate(src, cnt, feat, weight, adj, parts):
    outs = (jax.ShapeDtypeStruct((NZ, 256, HA), BF16),) + tuple(jax.ShapeDtypeStruct((256, HB), BF16) for _ in HOPS)
    return pl.pallas_call(
        aggregate_kernel,
        out_shape=outs,
        in_specs=[SMEM] * 2 + [VMEM] * 3 + [pl.BlockSpec(memory_space=pltpu.HBM)] * 3,
        out_specs=tuple(VMEM for _ in outs),
        scratch_shapes=[
            pltpu.VMEM((256, HB), BF16),
            pltpu.VMEM((4 * PART, BLK, HID), BF16),
            pltpu.SemaphoreType.DMA((3,)),
        ],
        compiler_params=pltpu.CompilerParams(vmem_limit_bytes=24 << 20),
        cost_estimate=pl.CostEstimate(flops=6 << 30, transcendentals=0, bytes_accessed=20 << 20),
    )(src, cnt, feat, weight, adj, *parts)


def exchange(x, axes):
    return lax.all_to_all(x, axes, 0, 0, tiled=True)


def hop(x, dx, dy):
    pairs = [(i * NY + j, (i + dx) % NX * NY + (j ^ dy)) for i in range(NX) for j in range(NY)]
    return lax.ppermute(x, ("x", "yl"), pairs)


def layer(src_feat, tgt_feat, rel_weight, self_weight, adj_weight, adj_source, adj_count):
    swap = [(0, 1), (1, 0)]
    far = lax.ppermute(src_feat, "yh", swap)
    near = lax.ppermute(src_feat, "core", swap)
    diag = lax.ppermute(far, "core", swap)
    parts = []
    for feat in (src_feat, near, far):
        parts.append(transform(feat, rel_weight))
    out_a, *out_b = aggregate(
        jnp.transpose(adj_source[0]), adj_count, diag, rel_weight, adj_weight[0], parts
    )
    got_a = exchange(out_a, "z")
    got_b = [out_b[0]] + [hop(b, dx, dy) for b, (dx, dy) in zip(out_b[1:], HOPS[1:])]
    sum_a = got_a.astype(F32).sum(0).astype(BF16).reshape(NX * NY, ROWS, HA)
    sum_b = sum(b.astype(F32) for b in got_b).astype(BF16).reshape(NZ, ROWS, HB)
    last_a = exchange(sum_a, ("x", "yl"))
    last_b = exchange(sum_b, "z")
    end_a = last_a.astype(F32).sum(0)
    end_b = last_b.astype(F32).sum(0)
    summed = jnp.concatenate([end_a, end_b], axis=1)
    self_term = jnp.dot(tgt_feat, self_weight, preferred_element_type=F32)
    return jax.nn.relu(summed + self_term).astype(BF16)


def solution(mesh):
    fine = Mesh(mesh.devices.reshape(NZ, NX, NY, 2, 2), ("z", "x", "yl", "yh", "core"))
    src, tgt = ("z", "x", "yl"), ("yh", "core")
    return jax.shard_map(
        layer,
        mesh=fine,
        in_specs=(
            P(src + tgt, None),
            P(tgt + src, None),
            P(),
            P(),
            P(src, tgt, None, None, None),
            P(src, tgt, None),
            P(src, tgt),
        ),
        out_specs=P(tgt + src, None),
        check_vma=False,
    )
```

```python
import jax
import jax.numpy as jnp
from jax import lax
from jax.experimental import pallas as pl
from jax.experimental.pallas import tpu as pltpu
from jax.sharding import Mesh, PartitionSpec as P


HID = 1024
BLK = 128
REL = 3
NZ, NX, NY = 8, 4, 2
ROWS = 32
HA = 256
HB = 512
HC = HID - HA - HB
PLACE = (0, 12, 24)
F32 = jnp.float32
BF16 = jnp.bfloat16
SMEM = pl.BlockSpec(memory_space=pltpu.SMEM)
VMEM = pl.BlockSpec(memory_space=pltpu.VMEM)


def transform_rows(f_ref, w_ref, t_ref, base):
    def step(i, _):
        h = i // REL
        r = i - h * REL
        y = jnp.dot(f_ref[pl.ds(h * 2 * BLK, 2 * BLK), :], w_ref[r], preferred_element_type=F32)
        t_ref[pl.ds(base + i * 2, 2)] = y.astype(BF16).reshape(2, BLK, HID)
        return 0

    lax.fori_loop(0, f_ref.shape[0] // (2 * BLK) * REL, step, 0)


def transform_kernel(f_ref, w_ref, t_ref):
    transform_rows(f_ref, w_ref, t_ref, 0)


def transform(feat, weight):
    return pl.pallas_call(
        transform_kernel,
        out_shape=jax.ShapeDtypeStruct((REL * feat.shape[0] // BLK, BLK, HID), BF16),
        in_specs=[VMEM, VMEM],
        out_specs=VMEM,
        compiler_params=pltpu.CompilerParams(vmem_limit_bytes=8 << 20),
        cost_estimate=pl.CostEstimate(
            flops=2 * feat.size * HID * REL, transcendentals=0, bytes_accessed=8 << 20
        ),
    )(feat, weight)


def weighted_sum(t, src_ref, cnt_ref, me, adj_ref, t_ref):
    weights, picked = [], []
    for k in range(adj_ref.shape[1]):
        v = src_ref[k, t]
        r = lax.shift_right_logical(v, 4)
        j = lax.bitwise_and(v, 15)
        half = lax.bitwise_xor(lax.shift_right_logical(j, 1), me * 2)
        w = adj_ref[t, k]
        weights.append(jnp.where(k < cnt_ref[0, t], w, jnp.zeros_like(w)))
        picked.append(t_ref[half * 6 + r * 2 + lax.bitwise_and(j, 1)])
    return jnp.dot(
        jnp.concatenate(weights, axis=1), jnp.concatenate(picked, axis=0), preferred_element_type=F32
    ).astype(BF16)


def aggregate_kernel(src_ref, cnt_ref, f_ref, w_ref, adj_ref, *refs):
    n = len(PLACE)
    parts, a_ref, b_refs, c_refs, (both, t_ref, sems) = refs[:n], refs[n], refs[n + 1 : -5], refs[-5:-3], refs[-3:]
    copies = []
    for q, part in enumerate(parts):
        copies.append(pltpu.make_async_copy(part, t_ref.at[pl.ds(PLACE[q], part.shape[0])], sems.at[q]))
    for copy in copies:
        copy.start()
    transform_rows(f_ref, w_ref, t_ref, 48 - f_ref.shape[0] // BLK * REL)
    for copy in copies:
        copy.wait()
    me = lax.axis_index("yh") * 2 + lax.axis_index("core")
    x0, y0 = lax.axis_index("x"), lax.axis_index("yl")
    b0, b1, b3, b20, b21 = b_refs

    def step(z, _):
        for odd in range(2):
            got = weighted_sum(z * 2 + odd, src_ref, cnt_ref, me, adj_ref, t_ref)
            a_ref[z, odd * BLK : (odd + 1) * BLK, :] = got[:, :HA]
            both[odd * BLK : (odd + 1) * BLK, :] = got[:, HA:]
        at = pl.ds(pl.multiple_of(z * ROWS, ROWS), ROWS)
        for dx in range(NX):
            for dy in range(NY):
                to = lax.bitwise_and(x0 + dx, NX - 1) * NY + lax.bitwise_xor(y0, dy)
                rows = both[pl.ds(pl.multiple_of(to * ROWS, ROWS), ROWS), :]
                if dx == 2:
                    (b20, b21)[dy][at, :] = rows[:, :HB]
                else:
                    (b0, b1, None, b3)[dx][dy, at, :] = rows[:, :HB]
                c_refs[dy][dx, at, :] = rows[:, HB:]
        return 0

    lax.fori_loop(0, NZ, step, 0)


def aggregate(src, cnt, feat, weight, adj, parts):
    shapes = [(NZ, 256, HA)] + [(NY, 256, HB)] * 3 + [(256, HB)] * 2 + [(NX, 256, HC)] * 2
    return pl.pallas_call(
        aggregate_kernel,
        out_shape=tuple(jax.ShapeDtypeStruct(shape, BF16) for shape in shapes),
        in_specs=[SMEM] * 2 + [VMEM] * 3 + [pl.BlockSpec(memory_space=pltpu.HBM)] * len(parts),
        out_specs=tuple(VMEM for _ in shapes),
        scratch_shapes=[
            pltpu.VMEM((256, HB + HC), BF16),
            pltpu.VMEM((48, BLK, HID), BF16),
            pltpu.SemaphoreType.DMA((len(parts),)),
        ],
        compiler_params=pltpu.CompilerParams(vmem_limit_bytes=24 << 20),
        cost_estimate=pl.CostEstimate(flops=6 << 30, transcendentals=0, bytes_accessed=20 << 20),
    )(src, cnt, feat, weight, adj, *parts)


def local(kernel, shapes, *args):
    return pl.pallas_call(
        kernel,
        out_shape=tuple(jax.ShapeDtypeStruct(shape, BF16) for shape in shapes),
        in_specs=[VMEM] * len(args),
        out_specs=tuple(VMEM for _ in shapes),
        compiler_params=pltpu.CompilerParams(vmem_limit_bytes=8 << 20),
    )(*args)


def add(*values):
    total = values[0].astype(F32)
    for value in values[1:]:
        total += value.astype(F32)
    return total.astype(BF16)


def b_relay(b1, b3, left, right, up, down):
    up[0] = add(b1[0], left[...])
    up[1] = b1[1]
    down[0] = b3[0]
    down[1] = add(b3[1], right[...])


def b_meet(b0, left, right, keep, send):
    keep[...] = add(b0[0], left[0], right[0])
    send[...] = add(b0[1], left[1], right[1])


def c_split(c0, other, own, up, low, high, down):
    half = low.shape[0]
    own[...] = add(c0[0], other[0])
    up[...] = add(c0[1], other[1])
    low[...] = add(c0[2, :half], other[2, :half])
    high[...] = add(c0[2, half:], other[2, half:])
    down[...] = add(c0[3], other[3])


def c_relay(up, down, left, right, up_out, down_out):
    half = left.shape[0]
    up_out[:half] = add(up[:half], left[...])
    up_out[half:] = up[half:]
    down_out[:half] = down[:half]
    down_out[half:] = add(down[half:], right[...])


def join(keep, other, own, left, right, out):
    for z in range(NZ):
        rows = slice(z * ROWS, (z + 1) * ROWS)
        out[z, :, :HB] = add(keep[rows], other[rows])
        out[z, :, HB:] = add(own[rows], left[rows], right[rows])


def exchange(x, axes):
    return lax.all_to_all(x, axes, 0, 0, tiled=True)


def along_x(x, d):
    return lax.ppermute(x, "x", [(i, (i + d) % NX) for i in range(NX)])


def layer(src_feat, tgt_feat, rel_weight, self_weight, adj_weight, adj_source, adj_count):
    swap = [(0, 1), (1, 0)]
    far = []
    for f in (src_feat,):
        far.append(lax.ppermute(f, "yh", swap))
    near = lax.ppermute(src_feat, "core", swap)
    t_own = transform(src_feat, rel_weight)
    t_near = transform(near, rel_weight)
    diag, t_far, t_diag = [], [], []
    for f in far:
        diag.append(lax.ppermute(f, "core", swap))
        t_far.append(transform(f, rel_weight))
    for f in diag[:-1]:
        t_diag.append(transform(f, rel_weight))
    out_a, b0, b1, b3, b20, b21, c0, c1 = aggregate(
        jnp.transpose(adj_source[0]),
        adj_count,
        diag[-1],
        rel_weight,
        adj_weight[0],
        [t_own, t_near] + t_far + t_diag,
    )
    b_left, b_right = along_x(b20, 1), along_x(b21, -1)
    c_other = lax.ppermute(c1, "yl", swap)
    got_a = exchange(out_a, "z")
    b_up, b_down = local(b_relay, [(NY, 256, HB)] * 2, b1, b3, b_left, b_right)
    b_left, b_right = along_x(b_up, 1), along_x(b_down, -1)
    shapes = [(256, HC), (256, HC), (BLK, HC), (BLK, HC), (256, HC)]
    c_own, c_up, c_low, c_high, c_down = local(c_split, shapes, c0, c_other)
    c_left, c_right = along_x(c_low, 1), along_x(c_high, -1)
    c_up, c_down = local(c_relay, [(256, HC)] * 2, c_up, c_down, c_left, c_right)
    c_left, c_right = along_x(c_up, 1), along_x(c_down, -1)
    b_keep, b_send = local(b_meet, [(256, HB)] * 2, b0, b_left, b_right)
    b_other = lax.ppermute(b_send, "yl", swap)
    sum_a = got_a.astype(F32).sum(0).astype(BF16).reshape(NX * NY, ROWS, HA)
    last_a = exchange(sum_a, ("x", "yl"))
    (joined,) = local(join, [(NZ, ROWS, HB + HC)], b_keep, b_other, c_own, c_left, c_right)
    last_b = exchange(joined, "z")
    end_a = last_a.astype(F32).sum(0)
    end_b = last_b.astype(F32).sum(0)
    summed = jnp.concatenate([end_a, end_b], axis=1)
    self_term = jnp.dot(tgt_feat, self_weight, preferred_element_type=F32)
    return jax.nn.relu(summed + self_term).astype(BF16)


def solution(mesh):
    fine = Mesh(mesh.devices.reshape(NZ, NX, NY, 2, 2), ("z", "x", "yl", "yh", "core"))
    src, tgt = ("z", "x", "yl"), ("yh", "core")
    return jax.shard_map(
        layer,
        mesh=fine,
        in_specs=(
            P(src + tgt, None),
            P(tgt + src, None),
            P(),
            P(),
            P(src, tgt, None, None, None),
            P(src, tgt, None),
            P(src, tgt),
        ),
        out_specs=P(tgt + src, None),
        check_vma=False,
    )
```

```python
import jax
import jax.numpy as jnp
from jax import lax
from jax.experimental import pallas as pl
from jax.experimental.pallas import tpu as pltpu
from jax.sharding import Mesh, PartitionSpec as P


HID = 1024
BLK = 128
REL = 3
NZ, NX, NY = 8, 4, 2
ROWS = 32
HA = 256
HB = 512
HC = HID - HA - HB
PLACE = (0, 12, 24)
F32 = jnp.float32
BF16 = jnp.bfloat16
SMEM = pl.BlockSpec(memory_space=pltpu.SMEM)
VMEM = pl.BlockSpec(memory_space=pltpu.VMEM)


def transform_rows(f_ref, w_ref, t_ref, base):
    def step(i, _):
        h = i // REL
        r = i - h * REL
        y = jnp.dot(f_ref[pl.ds(h * 2 * BLK, 2 * BLK), :], w_ref[r], preferred_element_type=F32)
        t_ref[pl.ds(base + i * 2, 2)] = y.astype(BF16).reshape(2, BLK, HID)
        return 0

    lax.fori_loop(0, f_ref.shape[0] // (2 * BLK) * REL, step, 0)


def transform_kernel(f_ref, w_ref, t_ref):
    transform_rows(f_ref, w_ref, t_ref, 0)


def transform(feat, weight):
    return pl.pallas_call(
        transform_kernel,
        out_shape=jax.ShapeDtypeStruct((REL * feat.shape[0] // BLK, BLK, HID), BF16),
        in_specs=[VMEM, VMEM],
        out_specs=VMEM,
        compiler_params=pltpu.CompilerParams(vmem_limit_bytes=8 << 20),
        cost_estimate=pl.CostEstimate(
            flops=2 * feat.size * HID * REL, transcendentals=0, bytes_accessed=8 << 20
        ),
    )(feat, weight)


def weighted_sum(t, src_ref, cnt_ref, me, adj_ref, t_ref):
    weights, picked = [], []
    for k in range(adj_ref.shape[1]):
        v = src_ref[k, t]
        r = lax.shift_right_logical(v, 4)
        j = lax.bitwise_and(v, 15)
        half = lax.bitwise_xor(lax.shift_right_logical(j, 1), me * 2)
        w = adj_ref[t, k]
        weights.append(jnp.where(k < cnt_ref[0, t], w, jnp.zeros_like(w)))
        picked.append(t_ref[half * 6 + r * 2 + lax.bitwise_and(j, 1)])
    return jnp.dot(
        jnp.concatenate(weights, axis=1), jnp.concatenate(picked, axis=0), preferred_element_type=F32
    ).astype(BF16)


def aggregate_kernel(src_ref, cnt_ref, f_ref, w_ref, adj_ref, *refs):
    n = len(PLACE)
    parts, (a_ref, low, high), b_refs = refs[:n], refs[n : n + 3], refs[n + 3 : -5]
    c_refs, (both, t_ref, sems) = refs[-5:-3], refs[-3:]
    copies = []
    for q, part in enumerate(parts):
        copies.append(pltpu.make_async_copy(part, t_ref.at[pl.ds(PLACE[q], part.shape[0])], sems.at[q]))
    for copy in copies:
        copy.start()
    transform_rows(f_ref, w_ref, t_ref, 48 - f_ref.shape[0] // BLK * REL)
    for copy in copies:
        copy.wait()
    me = lax.axis_index("yh") * 2 + lax.axis_index("core")
    x0, y0, z0 = lax.axis_index("x"), lax.axis_index("yl"), lax.axis_index("z")
    b0, b1, b3, b20, b21 = b_refs

    def step(d, _):
        z = lax.bitwise_and(z0 + d, NZ - 1)
        for odd in range(2):
            got = weighted_sum(z * 2 + odd, src_ref, cnt_ref, me, adj_ref, t_ref)
            a_ref[d, odd * BLK : (odd + 1) * BLK, :] = got[:, :HA]

            @pl.when(d == NZ // 2)
            def _():
                (low, high)[odd][...] = got[:, :HA]

            both[odd * BLK : (odd + 1) * BLK, :] = got[:, HA:]
        at = pl.ds(pl.multiple_of(z * ROWS, ROWS), ROWS)
        for dx in range(NX):
            for dy in range(NY):
                to = lax.bitwise_and(x0 + dx, NX - 1) * NY + lax.bitwise_xor(y0, dy)
                rows = both[pl.ds(pl.multiple_of(to * ROWS, ROWS), ROWS), :]
                if dx == 2:
                    (b20, b21)[dy][at, :] = rows[:, :HB]
                else:
                    (b0, b1, None, b3)[dx][dy, at, :] = rows[:, :HB]
                c_refs[dy][dx, at, :] = rows[:, HB:]
        return 0

    lax.fori_loop(0, NZ, step, 0)


def aggregate(src, cnt, feat, weight, adj, parts):
    shapes = [(NZ, 256, HA), (BLK, HA), (BLK, HA)] + [(NY, 256, HB)] * 3 + [(256, HB)] * 2 + [(NX, 256, HC)] * 2
    return pl.pallas_call(
        aggregate_kernel,
        out_shape=tuple(jax.ShapeDtypeStruct(shape, BF16) for shape in shapes),
        in_specs=[SMEM] * 2 + [VMEM] * 3 + [pl.BlockSpec(memory_space=pltpu.HBM)] * len(parts),
        out_specs=tuple(VMEM for _ in shapes),
        scratch_shapes=[
            pltpu.VMEM((256, HB + HC), BF16),
            pltpu.VMEM((48, BLK, HID), BF16),
            pltpu.SemaphoreType.DMA((len(parts),)),
        ],
        compiler_params=pltpu.CompilerParams(vmem_limit_bytes=24 << 20),
        cost_estimate=pl.CostEstimate(flops=6 << 30, transcendentals=0, bytes_accessed=20 << 20),
    )(src, cnt, feat, weight, adj, *parts)


def local(kernel, shapes, *args):
    return pl.pallas_call(
        kernel,
        out_shape=tuple(jax.ShapeDtypeStruct(shape, BF16) for shape in shapes),
        in_specs=[VMEM] * len(args),
        out_specs=tuple(VMEM for _ in shapes),
        compiler_params=pltpu.CompilerParams(vmem_limit_bytes=8 << 20),
    )(*args)


def add(*values):
    total = values[0].astype(F32)
    for value in values[1:]:
        total += value.astype(F32)
    return total.astype(BF16)


def a_relay(away):
    def kernel(a, left, right, up, down):
        if left.shape[0] < up.shape[0]:
            half = left.shape[0]
            up[:half] = add(a[away, :half], left[...])
            up[half:] = a[away, half:]
            down[:half] = a[NZ - away, :half]
            down[half:] = add(a[NZ - away, half:], right[...])
        else:
            up[...] = add(a[away], left[...])
            down[...] = add(a[NZ - away], right[...])

    return kernel


def a_sum(a, left, right, *outs):
    x0, y0 = lax.axis_index("x"), lax.axis_index("yl")
    for dx, out in enumerate(outs):
        for dy in range(NY):
            to = lax.bitwise_and(x0 + dx, NX - 1) * NY + lax.bitwise_xor(y0, dy)
            rows = pl.ds(pl.multiple_of(to * ROWS, ROWS), ROWS)
            out[dy] = add(a[0, rows, :], left[rows, :], right[rows, :])


def a_meet(s0, s1, s2, s3, keep, send):
    keep[...] = add(s0[0], s1[0], s2[0], s3[0])
    send[...] = add(s0[1], s1[1], s2[1], s3[1])


def b_relay(b1, b3, left, right, up, down):
    up[0] = add(b1[0], left[...])
    up[1] = b1[1]
    down[0] = b3[0]
    down[1] = add(b3[1], right[...])


def b_meet(b0, left, right, keep, send):
    keep[...] = add(b0[0], left[0], right[0])
    send[...] = add(b0[1], left[1], right[1])


def c_split(c0, other, own, up, low, high, down):
    half = low.shape[0]
    own[...] = add(c0[0], other[0])
    up[...] = add(c0[1], other[1])
    low[...] = add(c0[2, :half], other[2, :half])
    high[...] = add(c0[2, half:], other[2, half:])
    down[...] = add(c0[3], other[3])


def c_relay(up, down, left, right, up_out, down_out):
    half = left.shape[0]
    up_out[:half] = add(up[:half], left[...])
    up_out[half:] = up[half:]
    down_out[:half] = down[:half]
    down_out[half:] = add(down[half:], right[...])


def join(keep, other, own, left, right, out):
    for z in range(NZ):
        rows = slice(z * ROWS, (z + 1) * ROWS)
        out[z, :, :HB] = add(keep[rows], other[rows])
        out[z, :, HB:] = add(own[rows], left[rows], right[rows])


def exchange(x, axes):
    return lax.all_to_all(x, axes, 0, 0, tiled=True)


def along_z(x, d):
    return lax.ppermute(x, "z", [(i, (i + d) % NZ) for i in range(NZ)])


def along_x(x, d):
    return lax.ppermute(x, "x", [(i, (i + d) % NX) for i in range(NX)])


def layer(src_feat, tgt_feat, rel_weight, self_weight, adj_weight, adj_source, adj_count):
    swap = [(0, 1), (1, 0)]
    far = []
    for f in (src_feat,):
        far.append(lax.ppermute(f, "yh", swap))
    near = lax.ppermute(src_feat, "core", swap)
    t_own = transform(src_feat, rel_weight)
    t_near = transform(near, rel_weight)
    diag, t_far, t_diag = [], [], []
    for f in far:
        diag.append(lax.ppermute(f, "core", swap))
        t_far.append(transform(f, rel_weight))
    for f in diag[:-1]:
        t_diag.append(transform(f, rel_weight))
    a, low, high, b0, b1, b3, b20, b21, c0, c1 = aggregate(
        jnp.transpose(adj_source[0]),
        adj_count,
        diag[-1],
        rel_weight,
        adj_weight[0],
        [t_own, t_near] + t_far + t_diag,
    )
    a_left, a_right = along_z(low, 1), along_z(high, -1)
    b_left, b_right = along_x(b20, 1), along_x(b21, -1)
    c_other = lax.ppermute(c1, "yl", swap)
    for away in (3, 2, 1):
        up, down = local(a_relay(away), [(256, HA)] * 2, a, a_left, a_right)
        a_left, a_right = along_z(up, 1), along_z(down, -1)
    b_up, b_down = local(b_relay, [(NY, 256, HB)] * 2, b1, b3, b_left, b_right)
    b_left, b_right = along_x(b_up, 1), along_x(b_down, -1)
    shapes = [(256, HC), (256, HC), (BLK, HC), (BLK, HC), (256, HC)]
    c_own, c_up, c_low, c_high, c_down = local(c_split, shapes, c0, c_other)
    c_left, c_right = along_x(c_low, 1), along_x(c_high, -1)
    b_keep, b_send = local(b_meet, [(256, HB)] * 2, b0, b_left, b_right)
    b_other = lax.ppermute(b_send, "yl", swap)
    c_up, c_down = local(c_relay, [(256, HC)] * 2, c_up, c_down, c_left, c_right)
    c_left, c_right = along_x(c_up, 1), along_x(c_down, -1)
    s0, s1, s2, s3 = local(a_sum, [(NY, ROWS, HA)] * NX, a, a_left, a_right)
    s1, s2, s3 = along_x(s1, 1), along_x(s2, 2), along_x(s3, 3)
    (joined,) = local(join, [(NZ, ROWS, HB + HC)], b_keep, b_other, c_own, c_left, c_right)
    last_b = exchange(joined, "z")
    a_keep, a_send = local(a_meet, [(ROWS, HA)] * 2, s0, s1, s2, s3)
    a_other = lax.ppermute(a_send, "yl", swap)
    end_a = a_keep.astype(F32) + a_other.astype(F32)
    end_b = last_b.astype(F32).sum(0)
    summed = jnp.concatenate([end_a, end_b], axis=1)
    self_term = jnp.dot(tgt_feat, self_weight, preferred_element_type=F32)
    return jax.nn.relu(summed + self_term).astype(BF16)


def solution(mesh):
    fine = Mesh(mesh.devices.reshape(NZ, NX, NY, 2, 2), ("z", "x", "yl", "yh", "core"))
    src, tgt = ("z", "x", "yl"), ("yh", "core")
    return jax.shard_map(
        layer,
        mesh=fine,
        in_specs=(
            P(src + tgt, None),
            P(tgt + src, None),
            P(),
            P(),
            P(src, tgt, None, None, None),
            P(src, tgt, None),
            P(src, tgt),
        ),
        out_specs=P(tgt + src, None),
        check_vma=False,
    )
```

```python
import jax
import jax.numpy as jnp
from jax import lax
from jax.experimental import pallas as pl
from jax.experimental.pallas import tpu as pltpu
from jax.sharding import Mesh, PartitionSpec as P


HID = 1024
BLK = 128
REL = 3
NZ, NX, NY = 8, 4, 2
ROWS = 32
HA = 384
HB = 384
HC = HID - HA - HB
PLACE = (0, 12, 24)
F32 = jnp.float32
BF16 = jnp.bfloat16
SMEM = pl.BlockSpec(memory_space=pltpu.SMEM)
VMEM = pl.BlockSpec(memory_space=pltpu.VMEM)


def transform_rows(f_ref, w_ref, t_ref, base):
    def step(i, _):
        h = i // REL
        r = i - h * REL
        y = jnp.dot(f_ref[pl.ds(h * 2 * BLK, 2 * BLK), :], w_ref[r], preferred_element_type=F32)
        t_ref[pl.ds(base + i * 2, 2)] = y.astype(BF16).reshape(2, BLK, HID)
        return 0

    lax.fori_loop(0, f_ref.shape[0] // (2 * BLK) * REL, step, 0)


def transform_kernel(f_ref, w_ref, t_ref):
    transform_rows(f_ref, w_ref, t_ref, 0)


def transform(feat, weight):
    return pl.pallas_call(
        transform_kernel,
        out_shape=jax.ShapeDtypeStruct((REL * feat.shape[0] // BLK, BLK, HID), BF16),
        in_specs=[VMEM, VMEM],
        out_specs=VMEM,
        compiler_params=pltpu.CompilerParams(vmem_limit_bytes=8 << 20),
        cost_estimate=pl.CostEstimate(
            flops=2 * feat.size * HID * REL, transcendentals=0, bytes_accessed=8 << 20
        ),
    )(feat, weight)


def weighted_sum(t, src_ref, cnt_ref, me, adj_ref, t_ref):
    weights, picked = [], []
    for k in range(adj_ref.shape[1]):
        v = src_ref[k, t]
        r = lax.shift_right_logical(v, 4)
        j = lax.bitwise_and(v, 15)
        half = lax.bitwise_xor(lax.shift_right_logical(j, 1), me * 2)
        w = adj_ref[t, k]
        weights.append(jnp.where(k < cnt_ref[0, t], w, jnp.zeros_like(w)))
        picked.append(t_ref[half * 6 + r * 2 + lax.bitwise_and(j, 1)])
    return jnp.dot(
        jnp.concatenate(weights, axis=1), jnp.concatenate(picked, axis=0), preferred_element_type=F32
    ).astype(BF16)


def aggregate_kernel(src_ref, cnt_ref, f_ref, w_ref, adj_ref, *refs):
    n = len(PLACE)
    parts, (a_ref, low, high), b_refs = refs[:n], refs[n : n + 3], refs[n + 3 : -5]
    c_refs, (both, t_ref, sems) = refs[-5:-3], refs[-3:]
    copies = []
    for q, part in enumerate(parts):
        copies.append(pltpu.make_async_copy(part, t_ref.at[pl.ds(PLACE[q], part.shape[0])], sems.at[q]))
    for copy in copies:
        copy.start()
    transform_rows(f_ref, w_ref, t_ref, 48 - f_ref.shape[0] // BLK * REL)
    for copy in copies:
        copy.wait()
    me = lax.axis_index("yh") * 2 + lax.axis_index("core")
    x0, y0, z0 = lax.axis_index("x"), lax.axis_index("yl"), lax.axis_index("z")
    b0, b1, b3, b20, b21 = b_refs

    def step(d, _):
        z = lax.bitwise_and(z0 + d, NZ - 1)
        for odd in range(2):
            got = weighted_sum(z * 2 + odd, src_ref, cnt_ref, me, adj_ref, t_ref)
            a_ref[d, odd * BLK : (odd + 1) * BLK, :] = got[:, :HA]

            @pl.when(d == NZ // 2)
            def _():
                (low, high)[odd][...] = got[:, :HA]

            both[odd * BLK : (odd + 1) * BLK, :] = got[:, HA:]
        at = pl.ds(pl.multiple_of(z * ROWS, ROWS), ROWS)
        for dx in range(NX):
            for dy in range(NY):
                to = lax.bitwise_and(x0 + dx, NX - 1) * NY + lax.bitwise_xor(y0, dy)
                rows = both[pl.ds(pl.multiple_of(to * ROWS, ROWS), ROWS), :]
                if dx == 2:
                    (b20, b21)[dy][at, :] = rows[:, :HB]
                else:
                    (b0, b1, None, b3)[dx][dy, at, :] = rows[:, :HB]
                c_refs[dy][dx, at, :] = rows[:, HB:]
        return 0

    lax.fori_loop(0, NZ, step, 0)


def aggregate(src, cnt, feat, weight, adj, parts):
    shapes = [(NZ, 256, HA), (BLK, HA), (BLK, HA)] + [(NY, 256, HB)] * 3 + [(256, HB)] * 2 + [(NX, 256, HC)] * 2
    return pl.pallas_call(
        aggregate_kernel,
        out_shape=tuple(jax.ShapeDtypeStruct(shape, BF16) for shape in shapes),
        in_specs=[SMEM] * 2 + [VMEM] * 3 + [pl.BlockSpec(memory_space=pltpu.HBM)] * len(parts),
        out_specs=tuple(VMEM for _ in shapes),
        scratch_shapes=[
            pltpu.VMEM((256, HB + HC), BF16),
            pltpu.VMEM((48, BLK, HID), BF16),
            pltpu.SemaphoreType.DMA((len(parts),)),
        ],
        compiler_params=pltpu.CompilerParams(vmem_limit_bytes=24 << 20),
        cost_estimate=pl.CostEstimate(flops=6 << 30, transcendentals=0, bytes_accessed=20 << 20),
    )(src, cnt, feat, weight, adj, *parts)


def finish(b, keep, other, self_term, out):
    total = self_term[:, :HA] + (keep[...].astype(F32) + other[...].astype(F32))
    out[:, :HA] = jnp.maximum(total, 0.0).astype(BF16)
    total = self_term[:, HA:]
    for z in range(NZ):
        total += b[z].astype(F32)
    out[:, HA:] = jnp.maximum(total, 0.0).astype(BF16)


def local(kernel, shapes, *args):
    return pl.pallas_call(
        kernel,
        out_shape=tuple(jax.ShapeDtypeStruct(shape, BF16) for shape in shapes),
        in_specs=[VMEM] * len(args),
        out_specs=tuple(VMEM for _ in shapes),
        compiler_params=pltpu.CompilerParams(vmem_limit_bytes=8 << 20),
    )(*args)


def add(*values):
    total = values[0].astype(F32)
    for value in values[1:]:
        total += value.astype(F32)
    return total.astype(BF16)


def a_relay(away):
    def kernel(a, left, right, up, down):
        if left.shape[0] < up.shape[0]:
            half = left.shape[0]
            up[:half] = add(a[away, :half], left[...])
            up[half:] = a[away, half:]
            down[:half] = a[NZ - away, :half]
            down[half:] = add(a[NZ - away, half:], right[...])
        else:
            up[...] = add(a[away], left[...])
            down[...] = add(a[NZ - away], right[...])

    return kernel


def a_sum(a, left, right, *outs):
    x0, y0 = lax.axis_index("x"), lax.axis_index("yl")
    for dx, out in enumerate(outs):
        for dy in range(NY):
            to = lax.bitwise_and(x0 + dx, NX - 1) * NY + lax.bitwise_xor(y0, dy)
            rows = pl.ds(pl.multiple_of(to * ROWS, ROWS), ROWS)
            out[dy] = add(a[0, rows, :], left[rows, :], right[rows, :])


def a_meet(s0, s1, s2, s3, keep, send):
    keep[...] = add(s0[0], s1[0], s2[0], s3[0])
    send[...] = add(s0[1], s1[1], s2[1], s3[1])


def b_relay(b1, b3, left, right, up, down):
    up[0] = add(b1[0], left[...])
    up[1] = b1[1]
    down[0] = b3[0]
    down[1] = add(b3[1], right[...])


def b_meet(b0, left, right, keep, send):
    keep[...] = add(b0[0], left[0], right[0])
    send[...] = add(b0[1], left[1], right[1])


def c_split(c0, other, own, up, low, high, down):
    half = low.shape[0]
    own[...] = add(c0[0], other[0])
    up[...] = add(c0[1], other[1])
    low[...] = add(c0[2, :half], other[2, :half])
    high[...] = add(c0[2, half:], other[2, half:])
    down[...] = add(c0[3], other[3])


def c_relay(up, down, left, right, up_out, down_out):
    half = left.shape[0]
    up_out[:half] = add(up[:half], left[...])
    up_out[half:] = up[half:]
    down_out[:half] = down[:half]
    down_out[half:] = add(down[half:], right[...])


def join(keep, other, own, left, right, out):
    for z in range(NZ):
        rows = slice(z * ROWS, (z + 1) * ROWS)
        out[z, :, :HB] = add(keep[rows], other[rows])
        out[z, :, HB:] = add(own[rows], left[rows], right[rows])


def exchange(x, axes):
    return lax.all_to_all(x, axes, 0, 0, tiled=True)


def along_z(x, d):
    return lax.ppermute(x, "z", [(i, (i + d) % NZ) for i in range(NZ)])


def along_x(x, d):
    return lax.ppermute(x, "x", [(i, (i + d) % NX) for i in range(NX)])


def layer(src_feat, tgt_feat, rel_weight, self_weight, adj_weight, adj_source, adj_count):
    swap = [(0, 1), (1, 0)]
    far = []
    for f in (src_feat,):
        far.append(lax.ppermute(f, "yh", swap))
    near = lax.ppermute(src_feat, "core", swap)
    self_term = jnp.dot(tgt_feat, self_weight, preferred_element_type=F32)
    t_own = transform(src_feat, rel_weight)
    t_near = transform(near, rel_weight)
    diag, t_far, t_diag = [], [], []
    for f in far:
        diag.append(lax.ppermute(f, "core", swap))
        t_far.append(transform(f, rel_weight))
    for f in diag[:-1]:
        t_diag.append(transform(f, rel_weight))
    a, low, high, b0, b1, b3, b20, b21, c0, c1 = aggregate(
        jnp.transpose(adj_source[0]),
        adj_count,
        diag[-1],
        rel_weight,
        adj_weight[0],
        [t_own, t_near] + t_far + t_diag,
    )
    a_left, a_right = along_z(low, 1), along_z(high, -1)
    b_left, b_right = along_x(b20, 1), along_x(b21, -1)
    c_other = lax.ppermute(c1, "yl", swap)
    for away in (3, 2, 1):
        up, down = local(a_relay(away), [(256, HA)] * 2, a, a_left, a_right)
        a_left, a_right = along_z(up, 1), along_z(down, -1)
    b_up, b_down = local(b_relay, [(NY, 256, HB)] * 2, b1, b3, b_left, b_right)
    b_left, b_right = along_x(b_up, 1), along_x(b_down, -1)
    shapes = [(256, HC), (256, HC), (BLK, HC), (BLK, HC), (256, HC)]
    c_own, c_up, c_low, c_high, c_down = local(c_split, shapes, c0, c_other)
    c_left, c_right = along_x(c_low, 1), along_x(c_high, -1)
    b_keep, b_send = local(b_meet, [(256, HB)] * 2, b0, b_left, b_right)
    b_other = lax.ppermute(b_send, "yl", swap)
    c_up, c_down = local(c_relay, [(256, HC)] * 2, c_up, c_down, c_left, c_right)
    c_left, c_right = along_x(c_up, 1), along_x(c_down, -1)
    s0, s1, s2, s3 = local(a_sum, [(NY, ROWS, HA)] * NX, a, a_left, a_right)
    s1, s2, s3 = along_x(s1, 1), along_x(s2, 2), along_x(s3, 3)
    (joined,) = local(join, [(NZ, ROWS, HB + HC)], b_keep, b_other, c_own, c_left, c_right)
    last_b = exchange(joined, "z")
    a_keep, a_send = local(a_meet, [(ROWS, HA)] * 2, s0, s1, s2, s3)
    a_other = lax.ppermute(a_send, "yl", swap)
    (out,) = local(finish, [(ROWS, HID)], last_b, a_keep, a_other, self_term)
    return out


def solution(mesh):
    fine = Mesh(mesh.devices.reshape(NZ, NX, NY, 2, 2), ("z", "x", "yl", "yh", "core"))
    src, tgt = ("z", "x", "yl"), ("yh", "core")
    return jax.shard_map(
        layer,
        mesh=fine,
        in_specs=(
            P(src + tgt, None),
            P(tgt + src, None),
            P(),
            P(),
            P(src, tgt, None, None, None),
            P(src, tgt, None),
            P(src, tgt),
        ),
        out_specs=P(tgt + src, None),
        check_vma=False,
    )
```

```python
import jax
import jax.numpy as jnp
from jax import lax
from jax.experimental import pallas as pl
from jax.experimental.pallas import tpu as pltpu
from jax.sharding import Mesh, PartitionSpec as P


HID = 1024
BLK = 128
REL = 3
NZ, NX, NY = 8, 4, 2
ROWS = 32
HA = 384
HB = 384
HC = HID - HA - HB
PLACE = (0, 12, 24)
F32 = jnp.float32
BF16 = jnp.bfloat16
SMEM = pl.BlockSpec(memory_space=pltpu.SMEM)
VMEM = pl.BlockSpec(memory_space=pltpu.VMEM)


def transform_rows(f_ref, w_ref, t_ref, base):
    n = f_ref.shape[0] // BLK

    def step(r, _):
        y = jnp.dot(f_ref[...], w_ref[r], preferred_element_type=F32)
        t_ref[pl.ds(base + r * n, n)] = y.astype(BF16).reshape(n, BLK, HID)
        return 0

    lax.fori_loop(0, REL, step, 0)


def transform_kernel(f_ref, w_ref, t_ref):
    transform_rows(f_ref, w_ref, t_ref, 0)


def transform(feat, weight):
    return pl.pallas_call(
        transform_kernel,
        out_shape=jax.ShapeDtypeStruct((REL * feat.shape[0] // BLK, BLK, HID), BF16),
        in_specs=[VMEM, VMEM],
        out_specs=VMEM,
        compiler_params=pltpu.CompilerParams(vmem_limit_bytes=8 << 20),
        cost_estimate=pl.CostEstimate(
            flops=2 * feat.size * HID * REL, transcendentals=0, bytes_accessed=8 << 20
        ),
    )(feat, weight)


def weighted_sum(t, src_ref, cnt_ref, me, adj_ref, t_ref):
    weights, picked = [], []
    for k in range(adj_ref.shape[1]):
        v = src_ref[k, t]
        r = lax.shift_right_logical(v, 4)
        j = lax.bitwise_and(v, 15)
        q = lax.bitwise_xor(lax.shift_right_logical(j, 2), me)
        w = adj_ref[t, k]
        weights.append(jnp.where(k < cnt_ref[0, t], w, jnp.zeros_like(w)))
        picked.append(t_ref[q * 12 + r * 4 + lax.bitwise_and(j, 3)])
    return jnp.dot(
        jnp.concatenate(weights, axis=1), jnp.concatenate(picked, axis=0), preferred_element_type=F32
    ).astype(BF16)


def aggregate_kernel(src_ref, cnt_ref, f_ref, w_ref, adj_ref, *refs):
    n = len(PLACE)
    parts, a_refs, b_refs = refs[:n], refs[n : n + NZ + 1], refs[n + NZ + 1 : -5]
    c_refs, (both, t_ref, sems) = refs[-5:-3], refs[-3:]
    copies = []
    for q, part in enumerate(parts):
        copies.append(pltpu.make_async_copy(part, t_ref.at[pl.ds(PLACE[q], part.shape[0])], sems.at[q]))
    for copy in copies:
        copy.start()
    transform_rows(f_ref, w_ref, t_ref, 48 - f_ref.shape[0] // BLK * REL)
    for copy in copies:
        copy.wait()
    me = lax.axis_index("yh") * 2 + lax.axis_index("core")
    x0, y0, z0 = lax.axis_index("x"), lax.axis_index("yl"), lax.axis_index("z")
    b0, b1, b3, b20, b21 = b_refs

    def step(d, _):
        z = lax.bitwise_and(z0 + d, NZ - 1)
        for odd in range(2):
            got = weighted_sum(z * 2 + odd, src_ref, cnt_ref, me, adj_ref, t_ref)
            for away in range(NZ):

                @pl.when(d == away)
                def _():
                    if away == NZ // 2:
                        a_refs[away + odd * (NZ // 2)][...] = got[:, :HA]
                    else:
                        a_refs[away][odd * BLK : (odd + 1) * BLK, :] = got[:, :HA]

            both[odd * BLK : (odd + 1) * BLK, :] = got[:, HA:]
        at = pl.ds(pl.multiple_of(z * ROWS, ROWS), ROWS)
        for dx in range(NX):
            for dy in range(NY):
                to = lax.bitwise_and(x0 + dx, NX - 1) * NY + lax.bitwise_xor(y0, dy)
                rows = both[pl.ds(pl.multiple_of(to * ROWS, ROWS), ROWS), :]
                if dx == 2:
                    (b20, b21)[dy][at, :] = rows[:, :HB]
                else:
                    (b0, b1, None, b3)[dx][dy, at, :] = rows[:, :HB]
                c_refs[dy][dx, at, :] = rows[:, HB:]
        return 0

    lax.fori_loop(0, NZ, step, 0)


def aggregate(src, cnt, feat, weight, adj, parts):
    shapes = [(BLK if away in (NZ // 2, NZ) else 256, HA) for away in range(NZ + 1)]
    shapes += [(NY, 256, HB)] * 3 + [(256, HB)] * 2 + [(NX, 256, HC)] * 2
    return pl.pallas_call(
        aggregate_kernel,
        out_shape=tuple(jax.ShapeDtypeStruct(shape, BF16) for shape in shapes),
        in_specs=[SMEM] * 2 + [VMEM] * 3 + [pl.BlockSpec(memory_space=pltpu.HBM)] * len(parts),
        out_specs=tuple(VMEM for _ in shapes),
        scratch_shapes=[
            pltpu.VMEM((256, HB + HC), BF16),
            pltpu.VMEM((48, BLK, HID), BF16),
            pltpu.SemaphoreType.DMA((len(parts),)),
        ],
        compiler_params=pltpu.CompilerParams(vmem_limit_bytes=24 << 20),
        cost_estimate=pl.CostEstimate(flops=6 << 30, transcendentals=0, bytes_accessed=20 << 20),
    )(src, cnt, feat, weight, adj, *parts)


def finish(b, keep, other, self_term, out):
    total = self_term[:, :HA] + (keep[...].astype(F32) + other[...].astype(F32))
    out[:, :HA] = jnp.maximum(total, 0.0).astype(BF16)
    total = self_term[:, HA:]
    for z in range(NZ):
        total += b[z].astype(F32)
    out[:, HA:] = jnp.maximum(total, 0.0).astype(BF16)


def local(kernel, shapes, *args):
    return pl.pallas_call(
        kernel,
        out_shape=tuple(jax.ShapeDtypeStruct(shape, BF16) for shape in shapes),
        in_specs=[VMEM] * len(args),
        out_specs=tuple(VMEM for _ in shapes),
        compiler_params=pltpu.CompilerParams(vmem_limit_bytes=8 << 20),
    )(*args)


def add(*values):
    total = values[0].astype(F32)
    for value in values[1:]:
        total += value.astype(F32)
    return total.astype(BF16)


def a_relay(a_up, a_down, left, right, up, down):
    half = left.shape[0]
    up[:half] = add(a_up[:half], left[...])
    if half < up.shape[0]:
        up[half:] = a_up[half:]
        down[:half] = a_down[:half]
        down[half:] = add(a_down[half:], right[...])
    else:
        down[...] = add(a_down[...], right[...])


def a_sum(a, left, right, *outs):
    x0, y0 = lax.axis_index("x"), lax.axis_index("yl")
    for dx, out in enumerate(outs):
        for dy in range(NY):
            to = lax.bitwise_and(x0 + dx, NX - 1) * NY + lax.bitwise_xor(y0, dy)
            rows = pl.ds(pl.multiple_of(to * ROWS, ROWS), ROWS)
            out[dy] = add(a[rows, :], left[rows, :], right[rows, :])


def a_meet(s0, s1, s2, s3, keep, send):
    keep[...] = add(s0[0], s1[0], s2[0], s3[0])
    send[...] = add(s0[1], s1[1], s2[1], s3[1])


def b_relay(b1, b3, left, right, up, down):
    up[0] = add(b1[0], left[...])
    up[1] = b1[1]
    down[0] = b3[0]
    down[1] = add(b3[1], right[...])


def b_meet(b0, left, right, keep, send):
    keep[...] = add(b0[0], left[0], right[0])
    send[...] = add(b0[1], left[1], right[1])


def c_split(c0, other, own, up, low, high, down):
    half = low.shape[0]
    own[...] = add(c0[0], other[0])
    up[...] = add(c0[1], other[1])
    low[...] = add(c0[2, :half], other[2, :half])
    high[...] = add(c0[2, half:], other[2, half:])
    down[...] = add(c0[3], other[3])


def c_relay(up, down, left, right, up_out, down_out):
    half = left.shape[0]
    up_out[:half] = add(up[:half], left[...])
    up_out[half:] = up[half:]
    down_out[:half] = down[:half]
    down_out[half:] = add(down[half:], right[...])


def join(keep, other, own, left, right, out):
    for z in range(NZ):
        rows = slice(z * ROWS, (z + 1) * ROWS)
        out[z, :, :HB] = add(keep[rows], other[rows])
        out[z, :, HB:] = add(own[rows], left[rows], right[rows])


def exchange(x, axes):
    return lax.all_to_all(x, axes, 0, 0, tiled=True)


def along_z(x, d):
    return lax.ppermute(x, "z", [(i, (i + d) % NZ) for i in range(NZ)])


def along_x(x, d):
    return lax.ppermute(x, "x", [(i, (i + d) % NX) for i in range(NX)])


def layer(src_feat, tgt_feat, rel_weight, self_weight, adj_weight, adj_source, adj_count):
    swap = [(0, 1), (1, 0)]
    far = []
    for f in (src_feat,):
        far.append(lax.ppermute(f, "yh", swap))
    near = lax.ppermute(src_feat, "core", swap)
    self_term = jnp.dot(tgt_feat, self_weight, preferred_element_type=F32)
    t_own = transform(src_feat, rel_weight)
    t_near = transform(near, rel_weight)
    diag, t_far, t_diag = [], [], []
    for f in far:
        diag.append(lax.ppermute(f, "core", swap))
        t_far.append(transform(f, rel_weight))
    for f in diag[:-1]:
        t_diag.append(transform(f, rel_weight))
    got = aggregate(
        jnp.transpose(adj_source[0]),
        adj_count,
        diag[-1],
        rel_weight,
        adj_weight[0],
        [t_own, t_near] + t_far + t_diag,
    )
    a, (b0, b1, b3, b20, b21, c0, c1) = got[: NZ + 1], got[NZ + 1 :]
    a_left, a_right = along_z(a[NZ // 2], 1), along_z(a[NZ], -1)
    b_left, b_right = along_x(b20, 1), along_x(b21, -1)
    c_other = lax.ppermute(c1, "yl", swap)
    for away in (3, 2, 1):
        up, down = local(a_relay, [(256, HA)] * 2, a[away], a[NZ - away], a_left, a_right)
        a_left, a_right = along_z(up, 1), along_z(down, -1)
    b_up, b_down = local(b_relay, [(NY, 256, HB)] * 2, b1, b3, b_left, b_right)
    b_left, b_right = along_x(b_up, 1), along_x(b_down, -1)
    shapes = [(256, HC), (256, HC), (BLK, HC), (BLK, HC), (256, HC)]
    c_own, c_up, c_low, c_high, c_down = local(c_split, shapes, c0, c_other)
    c_left, c_right = along_x(c_low, 1), along_x(c_high, -1)
    b_keep, b_send = local(b_meet, [(256, HB)] * 2, b0, b_left, b_right)
    b_other = lax.ppermute(b_send, "yl", swap)
    c_up, c_down = local(c_relay, [(256, HC)] * 2, c_up, c_down, c_left, c_right)
    c_left, c_right = along_x(c_up, 1), along_x(c_down, -1)
    s0, s1, s2, s3 = local(a_sum, [(NY, ROWS, HA)] * NX, a[0], a_left, a_right)
    s2 = along_x(s2, 2)
    s1, s3 = along_x(s1, 1), along_x(s3, 3)
    (joined,) = local(join, [(NZ, ROWS, HB + HC)], b_keep, b_other, c_own, c_left, c_right)
    last_b = exchange(joined, "z")
    a_keep, a_send = local(a_meet, [(ROWS, HA)] * 2, s0, s1, s2, s3)
    a_other = lax.ppermute(a_send, "yl", swap)
    (out,) = local(finish, [(ROWS, HID)], last_b, a_keep, a_other, self_term)
    return out


def solution(mesh):
    fine = Mesh(mesh.devices.reshape(NZ, NX, NY, 2, 2), ("z", "x", "yl", "yh", "core"))
    src, tgt = ("z", "x", "yl"), ("yh", "core")
    return jax.shard_map(
        layer,
        mesh=fine,
        in_specs=(
            P(src + tgt, None),
            P(tgt + src, None),
            P(),
            P(),
            P(src, tgt, None, None, None),
            P(src, tgt, None),
            P(src, tgt),
        ),
        out_specs=P(tgt + src, None),
        check_vma=False,
    )
```
